32 devices in a mesh: groups: 2 (over y), row: 4 (over z), col: 4 (over x, core).
Axes of the slice: x: 2, y: 2, z: 4, core: 2. Of those that a mesh axis runs over, the one named last changes fastest.
Arguments:
- green_starting_blocks: float32 [4, 128, 2048], P('groups', None, ('row', 'col')), parts along dimension 0, may hold values from -3 to 3
- fit_vectors: bfloat16 [256, 4096], P('groups'), parts along dimension 0, may hold values from -0.75 to 0.75
- history: bfloat16 [4, 2048, 2048], P('groups', 'row', 'col'), parts along dimension 0, may hold values from -0.125 to 0.125
Outputs:
- green_final: float32 [4, 128, 2048], P('groups', None, ('row', 'col')), parts along dimension 0
The draws below stay inside these ranges and needn't reach their ends.
There are 2 independent parts, one for each index of `groups`. The reference program is written for one: setup_inputs(seed, part) draws one part's arguments, and reference() takes and returns one part's arrays. A program takes and returns all parts, laid end to end along the dimension named above; each array names one. Nothing has to cross between parts.
All inputs are finite; a program needn't handle non-finite values.
Results may differ from the reference program's by a relative error of at most 0.03.
Values may be sent and summed in bfloat16 or wider, within the bound.
A program may use at most 128 MiB of HBM per device.

```python
import jax
import jax.numpy as jnp
from jax import lax

NO = 64
NAUX = 128
NEW = 2
ITERS = 2
PAST = 32
SLICE_ROWS = 128
ORDER = 2048


def strengthened(array, own_key, source, target, blocks, factor):
    owner, partner = [(jnp.arange(array.shape[axis_at]) // (array.shape[axis_at] // blocks)).reshape([-1 if axis == axis_at else 1 for axis in range(array.ndim)]) for axis_at in (source, target)]
    chosen = jax.random.permutation(own_key, blocks)[partner]
    strong = (owner == chosen) | (owner == (partner + blocks // 2) % blocks)
    return jnp.where(strong, factor * array, array)


def steps_of(key, shape, pieces, smallest, high):
    gain = 1.0
    for dim, blocks in pieces:
        steps = jax.random.uniform(jax.random.fold_in(jax.random.fold_in(key, 6), dim), (blocks,), jnp.float32, smallest / len(pieces), high / len(pieces))
        gain = gain * jnp.repeat(jnp.exp(steps), shape[dim] // blocks).reshape((-1,) + (1,) * (len(shape) - 1 - dim))
    return gain


def gaussian(rng, extent, spread, limit, split=(), kind=jnp.bfloat16):
    entries = spread * jax.random.normal(rng, extent, jnp.float32)
    if split:
        entries = entries * steps_of(rng, extent, split, -0.22, 0.18)
    return jnp.clip(entries, -limit, limit).astype(kind)


def bell_draw_with(own_key, extent, deviation, bound, split, heavy, kind=jnp.bfloat16):
    array = deviation * jax.random.normal(own_key, extent, jnp.float32)
    if split:
        array = array * steps_of(own_key, extent, split, -0.22, 0.18)
    return jnp.clip(strengthened(array, jax.random.fold_in(own_key, 3), *heavy), -bound, bound).astype(kind)


def setup_inputs(seed: int = 0, part: int = 0) -> dict:
    seeds = jax.random.split(jax.random.key(seed), 4)
    part_splits = jax.random.split(jax.random.fold_in(seeds[3], part), 4)
    return {
        "green_starting_blocks": gaussian(part_splits[0], (2, SLICE_ROWS, ORDER), 0.5, 3.0, ((2, 16),), jnp.float32),
        "fit_vectors": gaussian(part_splits[1], (NAUX, NO * NO), NO ** -0.5, 0.75),
        "history": bell_draw_with(part_splits[2], (2, ORDER, ORDER), (2 * ORDER) ** -0.5, 0.125, ((1, 4), (2, 4)), (1, 2, 4, 2.0)),
    }


def pair_self_energy(pair_blocks, fit_vectors):
    pair_count = pair_blocks.shape[1]
    orbitals = pair_blocks.shape[2]
    aux_count = fit_vectors.shape[0]
    lowered = pair_blocks.astype(jnp.bfloat16)
    fit_basis = fit_vectors.reshape(aux_count * orbitals, orbitals)
    inner_side = jnp.transpose(lowered, (2, 0, 1, 3)).reshape(orbitals, 2 * pair_count * orbitals)
    left_prod = jnp.dot(fit_basis, inner_side, preferred_element_type=jnp.float32).astype(jnp.bfloat16)
    left_prod = left_prod.reshape(aux_count, orbitals, 2, pair_count, orbitals)
    fit_turned = jnp.transpose(fit_vectors.reshape(aux_count, orbitals, orbitals), (1, 0, 2)).reshape(orbitals, aux_count * orbitals)
    right_prod = jnp.dot(lowered.reshape(2 * pair_count * orbitals, orbitals), fit_turned, preferred_element_type=jnp.float32).astype(jnp.bfloat16)
    right_prod = right_prod.reshape(2, pair_count, orbitals, aux_count, orbitals)
    bubble = jnp.einsum("picnk,cniqk->npq", left_prod.astype(jnp.float32), right_prod.astype(jnp.float32)) / orbitals
    bubble = bubble.astype(jnp.bfloat16)
    screened = jnp.einsum("npq,qm->npm", bubble.astype(jnp.float32), fit_vectors.astype(jnp.float32)).astype(jnp.bfloat16)
    screened = screened.reshape(pair_count, aux_count, orbitals, orbitals)
    scale_factor = (aux_count * orbitals) ** -0.5
    energy = jnp.einsum("picnl,nplj->cnij", left_prod.astype(jnp.float32), screened.astype(jnp.float32)) * scale_factor
    return energy.astype(jnp.bfloat16)


def reference(green_starting_blocks, fit_vectors, history):
    green_current = green_starting_blocks

    def per_time(time_block):
        return pair_self_energy(time_block, fit_vectors)

    for iteration in range(ITERS):
        time_blocks = green_current.reshape(2, NEW, NO, PAST, NO).transpose(3, 0, 1, 2, 4)
        energies = lax.map(per_time, time_blocks)
        self_energy = energies.transpose(1, 2, 3, 0, 4).reshape(2, SLICE_ROWS, ORDER)
        stacked = self_energy.reshape(2 * SLICE_ROWS, ORDER)
        real_half = jnp.dot(stacked, history[0], preferred_element_type=jnp.float32)
        imaginary_half = jnp.dot(stacked, history[1], preferred_element_type=jnp.float32)
        collision_real = real_half[:SLICE_ROWS] - imaginary_half[SLICE_ROWS:]
        collision_imaginary = imaginary_half[:SLICE_ROWS] + real_half[SLICE_ROWS:]
        green_current = green_starting_blocks + jnp.stack([collision_real, collision_imaginary])
    return green_current
```

```python
import functools

import jax
import jax.numpy as jnp
from jax import lax
from jax.experimental import pallas as pl
from jax.experimental.pallas import tpu as pltpu
from jax.sharding import PartitionSpec as P

NO = 64
NEW = 2
ITERS = 2
PITCH = NO + 8
SLOTS = 4
PAIR = 2 * NO
WIDE = SLOTS * NO
F32 = jnp.float32
BF16 = jnp.bfloat16
MESH = pl.DeviceIdType.MESH
VMEM = pl.BlockSpec(memory_space=pltpu.VMEM)


def mm(a, b):
    return jnp.dot(a, b, preferred_element_type=F32)


def mm_nt(a, b):
    return lax.dot_general(a, b, (((1,), (1,)), ((), ())), preferred_element_type=F32)


def prepare(fit_ref, fitt_ref, bt_ref, turned):
    for pair in range(NO // 2):
        at = slice(pair * PAIR, (pair + 1) * PAIR)
        block = fit_ref[:, at].astype(F32).T
        fitt_ref[at, :] = block.astype(BF16)
        for half in range(2):
            i = 2 * pair + half
            turned[i * PITCH : i * PITCH + NO, :] = block[half * NO : (half + 1) * NO]
    for pair in range(NO // 2):
        pieces = [turned[pl.ds(2 * pair + half, NO, stride=PITCH), :] for half in range(2)]
        bt_ref[:, pair * PAIR : (pair + 1) * PAIR] = jnp.concatenate(pieces, axis=0).T.astype(BF16)


def places(sel_ref):
    shape = (PAIR, 2 * PAIR)
    row = lax.broadcasted_iota(jnp.int32, shape, 0)
    lane = lax.broadcasted_iota(jnp.int32, shape, 1)
    c, i = row // NO, row % NO
    for q in range(2):
        k = c * PAIR + (i // SLOTS) * (2 * SLOTS) + q * SLOTS + i % SLOTS
        sel_ref[q] = jnp.where(lane == k, 1.0, 0.0).astype(BF16)


def lay_out(a, now_ref, sel_ref, slotted, slot_ref, turn_ref):
    span = now_ref.shape[2]
    rows = 2 * span * SLOTS
    lane = lax.broadcasted_iota(jnp.int32, (span, PAIR), 1)
    blocks = [now_ref[c, a * NO : (a + 1) * NO, :] for c in range(2)]
    for c in range(2):
        both = jnp.concatenate([blocks[c], blocks[c]], axis=0).T
        halves = [jnp.where(lane < NO, both, 0.0), jnp.where(lane >= NO, both, 0.0)]
        for s in range(SLOTS):
            slotted[pl.ds((s // 2) * rows + c * span * SLOTS + s, span, stride=SLOTS), :] = halves[s % 2]
    for half in range(2):
        slot_ref[:, half * PAIR : (half + 1) * PAIR] = slotted[half * rows : (half + 1) * rows, :].astype(BF16)
    turned = jnp.concatenate(blocks, axis=0).T.astype(BF16)
    for q in range(2):
        turn_ref[q] = mm(turned, sel_ref[q]).astype(BF16)


def left(fit_ref, slot_ref, m_ref):
    aux = fit_ref.shape[0]
    for t in range(NO // (2 * SLOTS)):
        at = 2 * t * WIDE
        weights = jnp.concatenate([fit_ref[:, at : at + WIDE], fit_ref[:, at + WIDE : at + 2 * WIDE]], axis=0)
        res = mm_nt(slot_ref[...], weights)
        parts = [res[:, h * aux : (h + 1) * aux].reshape(-1, 2 * SLOTS, aux) for h in range(2)]
        m_ref[:, 4 * SLOTS * t : 4 * SLOTS * (t + 1), :] = jnp.concatenate(parts, axis=1).astype(BF16)


def pair_tile(m_ref, times, n, pair):
    pairs = NO // 2
    return jnp.concatenate([m_ref[(c * times + n) * pairs + pair] for c in range(2)], axis=0)


def contract(times, fitt_ref, bt_ref, sel_ref, turn_ref, m_ref, x_ref, w_ref):
    aux = fitt_ref.shape[1]
    for n in range(times):
        lhs = jnp.concatenate([turn_ref[q, n * NO : (n + 1) * NO, :] for q in range(2)], axis=0)
        for u in range(NO // 4):
            pairs = [2 * u, 2 * u + 1]
            res = mm(lhs, jnp.concatenate([pair_tile(m_ref, times, n, p) for p in pairs], axis=1)).astype(BF16)
            for d, p in enumerate(pairs):
                x_ref[p * PAIR : (p + 1) * PAIR, n * aux : (n + 1) * aux] = res[:, d * aux : (d + 1) * aux]

    pi = (mm(bt_ref[...], x_ref[...]) * (1.0 / NO)).astype(BF16)

    for step in range(NO * NO // 512):
        at = slice(step * 512, (step + 1) * 512)
        w_ref[at, :] = mm(fitt_ref[at, :], pi).astype(BF16)

    scale = (aux * NO) ** (-0.5)
    lane = lax.broadcasted_iota(jnp.int32, (NO, 2 * PAIR), 1)
    first = lane % (2 * SLOTS) < SLOTS
    sums = []
    for n in range(times):
        lanes = slice(n * aux, (n + 1) * aux)
        acc = jnp.zeros((PAIR, 2 * PAIR), F32)
        for u in range(NO // 4):
            pairs = [2 * u, 2 * u + 1]
            lhs = jnp.concatenate([w_ref[p * PAIR : (p + 1) * PAIR, lanes] for p in pairs], axis=1)
            rhs = jnp.concatenate([pair_tile(m_ref, times, n, p) for p in pairs], axis=1)
            acc = acc + mm_nt(lhs, rhs)
        sums.append(jnp.where(first, acc[:NO], acc[NO:]))
    total = jnp.concatenate(sums, axis=0) * scale
    high = total.astype(BF16)
    low = (total - high.astype(F32)).astype(BF16)
    fold = sel_ref[0] + sel_ref[1]
    return (mm_nt(fold, high) + mm_nt(fold, low)).astype(BF16)


def whole_kernel(
    rows_n, cols_n, green_ref, fit_ref, hist_ref, out_ref,
    fitt, bt, turned, sel, slotted, slot_ref, turn_ref, m_ref, x_ref, w_ref,
    now, energy, seg, part, got, gs_sem, gr_sem, ss_sem, sr_sem,
):
    row, col = lax.axis_index("row"), lax.axis_index("col")
    span = green_ref.shape[2]
    times = span // NO
    source_col = (row * cols_n + col) // rows_n

    def owner(m):
        t = col * rows_n + m
        return t // cols_n, lax.rem(t, cols_n)

    def away(m):
        to_row, to_col = owner(m)
        return jnp.logical_or(to_row != row, to_col != col)

    def foreign(r):
        return jnp.logical_or(row != r, col != source_col)

    def place(r, c):
        return {"row": r, "col": c}

    barrier = pltpu.get_barrier_semaphore()
    for d in range(1, cols_n):
        pl.semaphore_signal(barrier, inc=1, device_id=place(row, lax.rem(col + d, cols_n)), device_id_type=MESH)
    for r in range(rows_n):

        @pl.when(foreign(r))
        def _():
            pl.semaphore_signal(barrier, inc=1, device_id=place(r, source_col), device_id_type=MESH)

    slotted[...] = jnp.zeros_like(slotted)
    places(sel)
    prepare(fit_ref, fitt, bt, turned)

    keeps = jnp.where(source_col == col, 1, 0)
    pl.semaphore_wait(barrier, cols_n - 1 + rows_n - keeps)

    def gather(s, d):
        return pltpu.make_async_remote_copy(
            src_ref=energy.at[s],
            dst_ref=seg.at[s, col],
            send_sem=gs_sem.at[s, d],
            recv_sem=gr_sem.at[s, d],
            device_id=place(row, lax.rem(col + d, cols_n)),
            device_id_type=MESH,
        )

    def scatter(s, m):
        return pltpu.make_async_remote_copy(
            src_ref=part.at[s, m],
            dst_ref=got.at[s, row],
            send_sem=ss_sem.at[s, m],
            recv_sem=sr_sem.at[s, row],
            device_id=place(*owner(m)),
            device_id_type=MESH,
        )

    def arriving(s, r):
        return pltpu.make_async_remote_copy(
            src_ref=part.at[s, r],
            dst_ref=got.at[s, r],
            send_sem=ss_sem.at[s, r],
            recv_sem=sr_sem.at[s, r],
            device_id=place(r, source_col),
            device_id_type=MESH,
        )

    def keep(s, m):
        return pltpu.make_async_copy(part.at[s, m], got.at[s, row], sr_sem.at[s, row])

    def multiply(s):
        for d in range(1, cols_n):
            gather(s, d).wait_recv()
        real = [seg[s, q, :NO, :] for q in range(cols_n)]
        imag = [seg[s, q, NO:, :] for q in range(cols_n)]
        lhs = jnp.concatenate(
            [jnp.concatenate(real + [-x for x in imag], axis=1), jnp.concatenate(imag + real, axis=1)], axis=0
        )
        for m in range(rows_n):
            part[s, m] = mm(lhs, hist_ref[:, m * span : (m + 1) * span]).astype(BF16)
        for m in range(rows_n):

            @pl.when(away(m))
            def _():
                scatter(s, m).start()

            @pl.when(jnp.logical_not(away(m)))
            def _():
                keep(s, m).start()

    def collect(s, target):
        a = s % NEW
        for r in range(rows_n):

            @pl.when(foreign(r))
            def _():
                arriving(s, r).wait_recv()

            @pl.when(jnp.logical_not(foreign(r)))
            def _():
                keep(s, r).wait()

        total = got[s, 0].astype(F32)
        for r in range(1, rows_n):
            total = total + got[s, r].astype(F32)
        for c in range(2):
            at = slice(a * NO, (a + 1) * NO)
            target[c, at, :] = green_ref[c, at, :] + total[c * NO : (c + 1) * NO]

    steps = ITERS * NEW
    for s in range(steps):
        a = s % NEW
        if s >= NEW:
            collect(s - NEW, now)
        lay_out(a, green_ref if s < NEW else now, sel, slotted, slot_ref, turn_ref)
        left(fit_ref, slot_ref, m_ref)
        if s >= 1:
            multiply(s - 1)
        value = contract(times, fitt, bt, sel, turn_ref, m_ref, x_ref, w_ref)
        energy[s] = value
        for d in range(1, cols_n):
            gather(s, d).start()
        seg[s, col] = value
    multiply(steps - 1)
    for s in range(steps - NEW, steps):
        collect(s, out_ref)
    for s in range(steps):
        for d in range(1, cols_n):
            gather(s, d).wait_send()
        for m in range(rows_n):

            @pl.when(away(m))
            def _():
                scatter(s, m).wait_send()


def local(green, fit, history):
    rows_n, cols_n = lax.axis_size("row"), lax.axis_size("col")
    aux = fit.shape[0]
    span = green.shape[2]
    times = span // NO
    steps = ITERS * NEW
    stacked = history.reshape(2 * history.shape[1], history.shape[2])
    block = (2 * NO, span)
    return pl.pallas_call(
        functools.partial(whole_kernel, rows_n, cols_n),
        out_shape=jax.ShapeDtypeStruct(green.shape, F32),
        in_specs=[VMEM] * 3,
        out_specs=VMEM,
        scratch_shapes=[
            pltpu.VMEM((NO * NO, aux), BF16),
            pltpu.VMEM((aux, NO * NO), BF16),
            pltpu.VMEM((NO * PITCH, aux), F32),
            pltpu.VMEM((2, PAIR, 2 * PAIR), BF16),
            pltpu.VMEM((2 * 2 * span * SLOTS, PAIR), F32),
            pltpu.VMEM((2 * span * SLOTS, WIDE), BF16),
            pltpu.VMEM((2, span, 2 * PAIR), BF16),
            pltpu.VMEM((span, PAIR, aux), BF16),
            pltpu.VMEM((NO * NO, times * aux), BF16),
            pltpu.VMEM((NO * NO, times * aux), BF16),
            pltpu.VMEM(green.shape, F32),
            pltpu.VMEM((steps, *block), BF16),
            pltpu.VMEM((steps, cols_n, *block), BF16),
            pltpu.VMEM((steps, rows_n, *block), BF16),
            pltpu.VMEM((steps, rows_n, *block), BF16),
            pltpu.SemaphoreType.DMA((steps, cols_n)),
            pltpu.SemaphoreType.DMA((steps, cols_n)),
            pltpu.SemaphoreType.DMA((steps, rows_n)),
            pltpu.SemaphoreType.DMA((steps, rows_n)),
        ],
        compiler_params=pltpu.CompilerParams(
            collective_id=0, has_side_effects=True, vmem_limit_bytes=62 << 20
        ),
        name="whole",
    )(green, fit, stacked)


def solution(mesh):
    in_specs = (P("groups", None, ("row", "col")), P("groups", None), P("groups", "row", "col"))
    out_specs = P("groups", None, ("row", "col"))
    return jax.shard_map(local, mesh=mesh, in_specs=in_specs, out_specs=out_specs, check_vma=False)
```

```python
import functools

import jax
import jax.numpy as jnp
from jax import lax
from jax.experimental import pallas as pl
from jax.experimental.pallas import tpu as pltpu
from jax.sharding import PartitionSpec as P

NO = 64
NEW = 2
ITERS = 2
PITCH = NO + 8
SLOTS = 4
PAIR = 2 * NO
WIDE = SLOTS * NO
LEFTS = NO // (2 * SLOTS)
F32 = jnp.float32
BF16 = jnp.bfloat16
MESH = pl.DeviceIdType.MESH
VMEM = pl.BlockSpec(memory_space=pltpu.VMEM)


def mm(a, b):
    return jnp.dot(a, b, preferred_element_type=F32)


def mm_nt(a, b):
    return lax.dot_general(a, b, (((1,), (1,)), ((), ())), preferred_element_type=F32)


def prepare(piece, pieces, fit_ref, fitt_ref, bt_ref, turned):
    half_way = pieces // 2
    share = NO // 2 // half_way
    if piece < half_way:
        for pair in range(piece * share, (piece + 1) * share):
            at = slice(pair * PAIR, (pair + 1) * PAIR)
            block = fit_ref[:, at].astype(F32).T
            fitt_ref[at, :] = block.astype(BF16)
            for half in range(2):
                i = 2 * pair + half
                turned[i * PITCH : i * PITCH + NO, :] = block[half * NO : (half + 1) * NO]
        return
    for pair in range((piece - half_way) * share, (piece - half_way + 1) * share):
        rows = [turned[pl.ds(2 * pair + half, NO, stride=PITCH), :] for half in range(2)]
        bt_ref[:, pair * PAIR : (pair + 1) * PAIR] = jnp.concatenate(rows, axis=0).T.astype(BF16)


def places(sel_ref):
    shape = (PAIR, 2 * PAIR)
    row = lax.broadcasted_iota(jnp.int32, shape, 0)
    lane = lax.broadcasted_iota(jnp.int32, shape, 1)
    c, i = row // NO, row % NO
    for q in range(2):
        k = c * PAIR + (i // SLOTS) * (2 * SLOTS) + q * SLOTS + i % SLOTS
        sel_ref[q] = jnp.where(lane == k, 1.0, 0.0).astype(BF16)


def lay_out(a, now_ref, sel_ref, slotted, slot_ref, turn_ref):
    span = now_ref.shape[2]
    rows = 2 * span * SLOTS
    lane = lax.broadcasted_iota(jnp.int32, (span, PAIR), 1)
    blocks = [now_ref[c, a * NO : (a + 1) * NO, :] for c in range(2)]
    for c in range(2):
        both = jnp.concatenate([blocks[c], blocks[c]], axis=0).T
        halves = [jnp.where(lane < NO, both, 0.0), jnp.where(lane >= NO, both, 0.0)]
        for s in range(SLOTS):
            slotted[pl.ds((s // 2) * rows + c * span * SLOTS + s, span, stride=SLOTS), :] = halves[s % 2]
    for half in range(2):
        slot_ref[:, half * PAIR : (half + 1) * PAIR] = slotted[half * rows : (half + 1) * rows, :].astype(BF16)
    turned = jnp.concatenate(blocks, axis=0).T.astype(BF16)
    for q in range(2):
        turn_ref[q] = mm(turned, sel_ref[q]).astype(BF16)


def left(fit_ref, slot_ref, m_ref, beside):
    aux = fit_ref.shape[0]
    for t in range(LEFTS):
        at = 2 * t * WIDE
        weights = jnp.concatenate([fit_ref[:, at : at + WIDE], fit_ref[:, at + WIDE : at + 2 * WIDE]], axis=0)
        res = mm_nt(slot_ref[...], weights)
        parts = [res[:, h * aux : (h + 1) * aux].reshape(-1, 2 * SLOTS, aux) for h in range(2)]
        m_ref[:, 4 * SLOTS * t : 4 * SLOTS * (t + 1), :] = jnp.concatenate(parts, axis=1).astype(BF16)
        if beside is not None:
            beside(t)


def pair_tile(m_ref, times, n, pair):
    pairs = NO // 2
    return jnp.concatenate([m_ref[(c * times + n) * pairs + pair] for c in range(2)], axis=0)


def polarise(times, bt_ref, turn_ref, m_ref, x_ref):
    aux = bt_ref.shape[0]
    for n in range(times):
        lhs = jnp.concatenate([turn_ref[q, n * NO : (n + 1) * NO, :] for q in range(2)], axis=0)
        for u in range(NO // 4):
            pairs = [2 * u, 2 * u + 1]
            res = mm(lhs, jnp.concatenate([pair_tile(m_ref, times, n, p) for p in pairs], axis=1)).astype(BF16)
            for d, p in enumerate(pairs):
                x_ref[p * PAIR : (p + 1) * PAIR, n * aux : (n + 1) * aux] = res[:, d * aux : (d + 1) * aux]

    return (mm(bt_ref[...], x_ref[...]) * (1.0 / NO)).astype(BF16)


def dress(times, pi, fitt_ref, sel_ref, m_ref, w_ref):
    aux = fitt_ref.shape[1]
    for step in range(NO * NO // 512):
        at = slice(step * 512, (step + 1) * 512)
        w_ref[at, :] = mm(fitt_ref[at, :], pi).astype(BF16)

    scale = (aux * NO) ** (-0.5)
    lane = lax.broadcasted_iota(jnp.int32, (NO, 2 * PAIR), 1)
    first = lane % (2 * SLOTS) < SLOTS
    sums = []
    for n in range(times):
        lanes = slice(n * aux, (n + 1) * aux)
        acc = jnp.zeros((PAIR, 2 * PAIR), F32)
        for u in range(NO // 4):
            pairs = [2 * u, 2 * u + 1]
            lhs = jnp.concatenate([w_ref[p * PAIR : (p + 1) * PAIR, lanes] for p in pairs], axis=1)
            rhs = jnp.concatenate([pair_tile(m_ref, times, n, p) for p in pairs], axis=1)
            acc = acc + mm_nt(lhs, rhs)
        sums.append(jnp.where(first, acc[:NO], acc[NO:]))
    total = jnp.concatenate(sums, axis=0) * scale
    high = total.astype(BF16)
    low = (total - high.astype(F32)).astype(BF16)
    fold = sel_ref[0] + sel_ref[1]
    return (mm_nt(fold, high) + mm_nt(fold, low)).astype(BF16)


def whole_kernel(
    rows_n, cols_n, green_ref, fit_ref, hist_hbm, out_ref, hist_ref, load_sem,
    fitt, bt, turned, sel, slotted, slot_ref, turn_ref, m_ref, x_ref, w_ref,
    now, energy, seg, part, got, gs_sem, gr_sem, ss_sem, sr_sem,
):
    row, col = lax.axis_index("row"), lax.axis_index("col")
    span = green_ref.shape[2]
    times = span // NO
    source_col = (row * cols_n + col) // rows_n

    def owner(m):
        t = col * rows_n + m
        return t // cols_n, lax.rem(t, cols_n)

    def away(m):
        to_row, to_col = owner(m)
        return jnp.logical_or(to_row != row, to_col != col)

    def foreign(r):
        return jnp.logical_or(row != r, col != source_col)

    def place(r, c):
        return {"row": r, "col": c}

    barrier = pltpu.get_barrier_semaphore()
    for d in range(1, cols_n):
        pl.semaphore_signal(barrier, inc=1, device_id=place(row, lax.rem(col + d, cols_n)), device_id_type=MESH)
    for r in range(rows_n):

        @pl.when(foreign(r))
        def _():
            pl.semaphore_signal(barrier, inc=1, device_id=place(r, source_col), device_id_type=MESH)

    load = pltpu.make_async_copy(hist_hbm, hist_ref, load_sem)
    load.start()
    slotted[...] = jnp.zeros_like(slotted)
    places(sel)

    def gather(s, d):
        return pltpu.make_async_remote_copy(
            src_ref=energy.at[s],
            dst_ref=seg.at[s, col],
            send_sem=gs_sem.at[s, d],
            recv_sem=gr_sem.at[s, d],
            device_id=place(row, lax.rem(col + d, cols_n)),
            device_id_type=MESH,
        )

    def scatter(s, m):
        return pltpu.make_async_remote_copy(
            src_ref=part.at[s, m],
            dst_ref=got.at[s, row],
            send_sem=ss_sem.at[s, m],
            recv_sem=sr_sem.at[s, row],
            device_id=place(*owner(m)),
            device_id_type=MESH,
        )

    def arriving(s, r):
        return pltpu.make_async_remote_copy(
            src_ref=part.at[s, r],
            dst_ref=got.at[s, r],
            send_sem=ss_sem.at[s, r],
            recv_sem=sr_sem.at[s, r],
            device_id=place(r, source_col),
            device_id_type=MESH,
        )

    def keep(s, m):
        return pltpu.make_async_copy(part.at[s, m], got.at[s, row], sr_sem.at[s, row])

    def multiply(s):
        for d in range(1, cols_n):
            gather(s, d).wait_recv()
        real = [seg[s, q, :NO, :] for q in range(cols_n)]
        imag = [seg[s, q, NO:, :] for q in range(cols_n)]
        lhs = jnp.concatenate(
            [jnp.concatenate(real + [-x for x in imag], axis=1), jnp.concatenate(imag + real, axis=1)], axis=0
        )
        group = 2 if rows_n % 2 == 0 else 1
        for m in range(0, rows_n, group):
            value = mm(lhs, hist_ref[:, m * span : (m + group) * span]).astype(BF16)
            for d in range(group):
                part[s, m + d] = value[:, d * span : (d + 1) * span]
        for m in range(rows_n):

            @pl.when(away(m))
            def _():
                scatter(s, m).start()

            @pl.when(jnp.logical_not(away(m)))
            def _():
                keep(s, m).start()

    def collect(s, target):
        a = s % NEW
        for r in range(rows_n):

            @pl.when(foreign(r))
            def _():
                arriving(s, r).wait_recv()

            @pl.when(jnp.logical_not(foreign(r)))
            def _():
                keep(s, r).wait()

        total = got[s, 0].astype(F32)
        for r in range(1, rows_n):
            total = total + got[s, r].astype(F32)
        for c in range(2):
            at = slice(a * NO, (a + 1) * NO)
            target[c, at, :] = green_ref[c, at, :] + total[c * NO : (c + 1) * NO]

    def beside(t):
        prepare(t, LEFTS, fit_ref, fitt, bt, turned)

    steps = ITERS * NEW
    for s in range(steps):
        a = s % NEW
        if s >= NEW:
            if a == 0:
                multiply(s - 1)
            collect(s - NEW, now)
        lay_out(a, green_ref if s < NEW else now, sel, slotted, slot_ref, turn_ref)
        left(fit_ref, slot_ref, m_ref, beside if s == 0 else None)
        pi = polarise(times, bt, turn_ref, m_ref, x_ref)
        if a > 0:
            if s == 1:
                load.wait()
            multiply(s - 1)
        value = dress(times, pi, fitt, sel, m_ref, w_ref)
        energy[s] = value
        if s == 0:
            keeps = jnp.where(source_col == col, 1, 0)
            pl.semaphore_wait(barrier, cols_n - 1 + rows_n - keeps)
        for d in range(1, cols_n):
            gather(s, d).start()
        seg[s, col] = value
    multiply(steps - 1)
    for s in range(steps - NEW, steps):
        collect(s, out_ref)
    for s in range(steps):
        for d in range(1, cols_n):
            gather(s, d).wait_send()
        for m in range(rows_n):

            @pl.when(away(m))
            def _():
                scatter(s, m).wait_send()


def local(green, fit, history):
    rows_n, cols_n = lax.axis_size("row"), lax.axis_size("col")
    aux = fit.shape[0]
    span = green.shape[2]
    times = span // NO
    steps = ITERS * NEW
    stacked = history.reshape(2 * history.shape[1], history.shape[2])
    block = (2 * NO, span)
    return pl.pallas_call(
        functools.partial(whole_kernel, rows_n, cols_n),
        out_shape=jax.ShapeDtypeStruct(green.shape, F32),
        in_specs=[VMEM, VMEM, pl.BlockSpec(memory_space=pl.ANY)],
        out_specs=VMEM,
        scratch_shapes=[
            pltpu.VMEM(stacked.shape, BF16),
            pltpu.SemaphoreType.DMA,
            pltpu.VMEM((NO * NO, aux), BF16),
            pltpu.VMEM((aux, NO * NO), BF16),
            pltpu.VMEM((NO * PITCH, aux), F32),
            pltpu.VMEM((2, PAIR, 2 * PAIR), BF16),
            pltpu.VMEM((2 * 2 * span * SLOTS, PAIR), F32),
            pltpu.VMEM((2 * span * SLOTS, WIDE), BF16),
            pltpu.VMEM((2, span, 2 * PAIR), BF16),
            pltpu.VMEM((span, PAIR, aux), BF16),
            pltpu.VMEM((NO * NO, times * aux), BF16),
            pltpu.VMEM((NO * NO, times * aux), BF16),
            pltpu.VMEM(green.shape, F32),
            pltpu.VMEM((steps, *block), BF16),
            pltpu.VMEM((steps, cols_n, *block), BF16),
            pltpu.VMEM((steps, rows_n, *block), BF16),
            pltpu.VMEM((steps, rows_n, *block), BF16),
            pltpu.SemaphoreType.DMA((steps, cols_n)),
            pltpu.SemaphoreType.DMA((steps, cols_n)),
            pltpu.SemaphoreType.DMA((steps, rows_n)),
            pltpu.SemaphoreType.DMA((steps, rows_n)),
        ],
        compiler_params=pltpu.CompilerParams(
            collective_id=0, has_side_effects=True, vmem_limit_bytes=62 << 20
        ),
        name="whole",
    )(green, fit, stacked)


def solution(mesh):
    in_specs = (P("groups", None, ("row", "col")), P("groups", None), P("groups", "row", "col"))
    out_specs = P("groups", None, ("row", "col"))
    return jax.shard_map(local, mesh=mesh, in_specs=in_specs, out_specs=out_specs, check_vma=False)
```

```python
import functools

import jax
import jax.numpy as jnp
from jax import lax
from jax.experimental import pallas as pl
from jax.experimental.pallas import tpu as pltpu
from jax.sharding import PartitionSpec as P

NO = 64
NEW = 2
ITERS = 2
PITCH = NO + 8
SLOTS = 4
PAIR = 2 * NO
WIDE = SLOTS * NO
LEFTS = NO // (2 * SLOTS)
F32 = jnp.float32
BF16 = jnp.bfloat16
MESH = pl.DeviceIdType.MESH
VMEM = pl.BlockSpec(memory_space=pltpu.VMEM)


def mm(a, b):
    return jnp.dot(a, b, preferred_element_type=F32)


def mm_nt(a, b):
    return lax.dot_general(a, b, (((1,), (1,)), ((), ())), preferred_element_type=F32)


def prepare(piece, pieces, fit_ref, fitt_ref, bt_ref, turned):
    half_way = pieces // 2
    share = NO // 2 // half_way
    if piece < half_way:
        for pair in range(piece * share, (piece + 1) * share):
            at = slice(pair * PAIR, (pair + 1) * PAIR)
            block = fit_ref[:, at].astype(F32).T
            fitt_ref[at, :] = block.astype(BF16)
            for half in range(2):
                i = 2 * pair + half
                turned[i * PITCH : i * PITCH + NO, :] = block[half * NO : (half + 1) * NO]
        return
    for pair in range((piece - half_way) * share, (piece - half_way + 1) * share):
        rows = [turned[pl.ds(2 * pair + half, NO, stride=PITCH), :] for half in range(2)]
        bt_ref[:, pair * PAIR : (pair + 1) * PAIR] = jnp.concatenate(rows, axis=0).T.astype(BF16)


def places(sel_ref):
    shape = (PAIR, 2 * PAIR)
    row = lax.broadcasted_iota(jnp.int32, shape, 0)
    lane = lax.broadcasted_iota(jnp.int32, shape, 1)
    c, i = row // NO, row % NO
    for q in range(2):
        k = c * PAIR + (i // SLOTS) * (2 * SLOTS) + q * SLOTS + i % SLOTS
        sel_ref[q] = jnp.where(lane == k, 1.0, 0.0).astype(BF16)


def lay_out(a, now_ref, sel_ref, slotted, slot_ref, turn_ref):
    span = now_ref.shape[2]
    rows = 2 * span * SLOTS
    lane = lax.broadcasted_iota(jnp.int32, (span, PAIR), 1)
    blocks = [now_ref[c, a * NO : (a + 1) * NO, :] for c in range(2)]
    for c in range(2):
        both = jnp.concatenate([blocks[c], blocks[c]], axis=0).T
        halves = [jnp.where(lane < NO, both, 0.0), jnp.where(lane >= NO, both, 0.0)]
        for s in range(SLOTS):
            slotted[pl.ds((s // 2) * rows + c * span * SLOTS + s, span, stride=SLOTS), :] = halves[s % 2]
    for half in range(2):
        slot_ref[:, half * PAIR : (half + 1) * PAIR] = slotted[half * rows : (half + 1) * rows, :].astype(BF16)
    turned = jnp.concatenate(blocks, axis=0).T.astype(BF16)
    for q in range(2):
        turn_ref[q] = mm(turned, sel_ref[q]).astype(BF16)


def left(fit_ref, slot_ref, m_ref, beside):
    aux = fit_ref.shape[0]
    for t in range(LEFTS):
        at = 2 * t * WIDE
        weights = jnp.concatenate([fit_ref[:, at : at + WIDE], fit_ref[:, at + WIDE : at + 2 * WIDE]], axis=0)
        res = mm_nt(slot_ref[...], weights)
        parts = [res[:, h * aux : (h + 1) * aux].reshape(-1, 2 * SLOTS, aux) for h in range(2)]
        m_ref[:, 4 * SLOTS * t : 4 * SLOTS * (t + 1), :] = jnp.concatenate(parts, axis=1).astype(BF16)
        if beside is not None:
            beside(t)


def pair_tile(m_ref, times, n, pair):
    pairs = NO // 2
    return jnp.concatenate([m_ref[(c * times + n) * pairs + pair] for c in range(2)], axis=0)


def polarise(times, bt_ref, turn_ref, m_ref, x_ref):
    aux = bt_ref.shape[0]
    for n in range(times):
        lhs = jnp.concatenate([turn_ref[q, n * NO : (n + 1) * NO, :] for q in range(2)], axis=0)
        for u in range(NO // 4):
            pairs = [2 * u, 2 * u + 1]
            res = mm(lhs, jnp.concatenate([pair_tile(m_ref, times, n, p) for p in pairs], axis=1)).astype(BF16)
            for d, p in enumerate(pairs):
                x_ref[p * PAIR : (p + 1) * PAIR, n * aux : (n + 1) * aux] = res[:, d * aux : (d + 1) * aux]

    half = NO * NO // 2
    value = mm(bt_ref[:, :half], x_ref[:half]) * (1.0 / NO) + mm(bt_ref[:, half:], x_ref[half:]) * (1.0 / NO)
    return value.astype(BF16)


def dress(times, pi, fitt_ref, sel_ref, m_ref, w_ref):
    aux = fitt_ref.shape[1]
    for step in range(NO * NO // 512):
        at = slice(step * 512, (step + 1) * 512)
        w_ref[at, :] = mm(fitt_ref[at, :], pi).astype(BF16)

    scale = (aux * NO) ** (-0.5)
    lane = lax.broadcasted_iota(jnp.int32, (NO, 2 * PAIR), 1)
    first = lane % (2 * SLOTS) < SLOTS
    sums = []
    for n in range(times):
        lanes = slice(n * aux, (n + 1) * aux)
        accs = []
        for h in range(2):
            acc = jnp.zeros((PAIR, 2 * PAIR), F32)
            for u in range(h * NO // 8, (h + 1) * NO // 8):
                pairs = [2 * u, 2 * u + 1]
                lhs = jnp.concatenate([w_ref[p * PAIR : (p + 1) * PAIR, lanes] for p in pairs], axis=1)
                rhs = jnp.concatenate([pair_tile(m_ref, times, n, p) for p in pairs], axis=1)
                acc = acc + mm_nt(lhs, rhs)
            accs.append(acc * scale)
        acc = accs[0] + accs[1]
        sums.append(jnp.where(first, acc[:NO], acc[NO:]))
    total = jnp.concatenate(sums, axis=0)
    high = total.astype(BF16)
    low = (total - high.astype(F32)).astype(BF16)
    fold = sel_ref[0] + sel_ref[1]
    return (mm_nt(fold, high) + mm_nt(fold, low)).astype(BF16)


def whole_kernel(
    rows_n, cols_n, green_ref, fit_ref, hist_hbm, out_ref, hist_ref, load_sem,
    fitt, bt, turned, sel, slotted, slot_ref, turn_ref, m_ref, x_ref, w_ref,
    now, energy, seg, part, got, gs_sem, gr_sem, ss_sem, sr_sem,
):
    row, col = lax.axis_index("row"), lax.axis_index("col")
    span = green_ref.shape[2]
    times = span // NO
    source_col = (row * cols_n + col) // rows_n

    def owner(m):
        t = col * rows_n + m
        return t // cols_n, lax.rem(t, cols_n)

    def away(m):
        to_row, to_col = owner(m)
        return jnp.logical_or(to_row != row, to_col != col)

    def foreign(r):
        return jnp.logical_or(row != r, col != source_col)

    def place(r, c):
        return {"row": r, "col": c}

    barrier = pltpu.get_barrier_semaphore()
    for d in range(1, cols_n):
        pl.semaphore_signal(barrier, inc=1, device_id=place(row, lax.rem(col + d, cols_n)), device_id_type=MESH)
    for r in range(rows_n):

        @pl.when(foreign(r))
        def _():
            pl.semaphore_signal(barrier, inc=1, device_id=place(r, source_col), device_id_type=MESH)

    load = pltpu.make_async_copy(hist_hbm, hist_ref, load_sem)
    load.start()
    slotted[...] = jnp.zeros_like(slotted)
    places(sel)

    def gather(s, d):
        return pltpu.make_async_remote_copy(
            src_ref=energy.at[s],
            dst_ref=seg.at[s, col],
            send_sem=gs_sem.at[s, d],
            recv_sem=gr_sem.at[s, d],
            device_id=place(row, lax.rem(col + d, cols_n)),
            device_id_type=MESH,
        )

    def scatter(s, m):
        return pltpu.make_async_remote_copy(
            src_ref=part.at[s, m],
            dst_ref=got.at[s, row],
            send_sem=ss_sem.at[s, m],
            recv_sem=sr_sem.at[s, row],
            device_id=place(*owner(m)),
            device_id_type=MESH,
        )

    def arriving(s, r):
        return pltpu.make_async_remote_copy(
            src_ref=part.at[s, r],
            dst_ref=got.at[s, r],
            send_sem=ss_sem.at[s, r],
            recv_sem=sr_sem.at[s, r],
            device_id=place(r, source_col),
            device_id_type=MESH,
        )

    def keep(s, m):
        return pltpu.make_async_copy(part.at[s, m], got.at[s, row], sr_sem.at[s, row])

    def multiply(s):
        for d in range(1, cols_n):
            gather(s, d).wait_recv()
        real = [seg[s, q, :NO, :] for q in range(cols_n)]
        imag = [seg[s, q, NO:, :] for q in range(cols_n)]
        sides = [
            jnp.concatenate([jnp.concatenate(real, axis=1), jnp.concatenate(imag, axis=1)], axis=0),
            jnp.concatenate([jnp.concatenate(imag, axis=1), jnp.concatenate([-x for x in real], axis=1)], axis=0),
        ]
        depth = cols_n * span
        group = 2 if rows_n % 2 == 0 else 1
        for m in range(0, rows_n, group):
            at = slice(m * span, (m + group) * span)
            value = (mm(sides[0], hist_ref[:depth, at]) - mm(sides[1], hist_ref[depth:, at])).astype(BF16)
            for d in range(group):
                part[s, m + d] = value[:, d * span : (d + 1) * span]
        for i in range(rows_n):
            m = lax.rem(row + i, rows_n)

            @pl.when(away(m))
            def _():
                scatter(s, m).start()

            @pl.when(jnp.logical_not(away(m)))
            def _():
                keep(s, m).start()

    def collect(s, target):
        a = s % NEW
        for r in range(rows_n):

            @pl.when(foreign(r))
            def _():
                arriving(s, r).wait_recv()

            @pl.when(jnp.logical_not(foreign(r)))
            def _():
                keep(s, r).wait()

        total = got[s, 0].astype(F32)
        for r in range(1, rows_n):
            total = total + got[s, r].astype(F32)
        for c in range(2):
            at = slice(a * NO, (a + 1) * NO)
            target[c, at, :] = green_ref[c, at, :] + total[c * NO : (c + 1) * NO]

    def beside(t):
        prepare(t, LEFTS, fit_ref, fitt, bt, turned)

    steps = ITERS * NEW
    for s in range(steps):
        a = s % NEW
        if s >= NEW:
            if a == 0:
                multiply(s - 1)
            collect(s - NEW, now)
        lay_out(a, green_ref if s < NEW else now, sel, slotted, slot_ref, turn_ref)
        left(fit_ref, slot_ref, m_ref, beside if s == 0 else None)
        pi = polarise(times, bt, turn_ref, m_ref, x_ref)
        if a > 0:
            if s == 1:
                load.wait()
            multiply(s - 1)
        value = dress(times, pi, fitt, sel, m_ref, w_ref)
        energy[s] = value
        if s == 0:
            keeps = jnp.where(source_col == col, 1, 0)
            pl.semaphore_wait(barrier, cols_n - 1 + rows_n - keeps)
        for d in range(1, cols_n):
            gather(s, d).start()
        seg[s, col] = value
    multiply(steps - 1)
    for s in range(steps - NEW, steps):
        collect(s, out_ref)
    for s in range(steps):
        for d in range(1, cols_n):
            gather(s, d).wait_send()
        for m in range(rows_n):

            @pl.when(away(m))
            def _():
                scatter(s, m).wait_send()


def local(green, fit, history):
    rows_n, cols_n = lax.axis_size("row"), lax.axis_size("col")
    aux = fit.shape[0]
    span = green.shape[2]
    times = span // NO
    steps = ITERS * NEW
    stacked = history.reshape(2 * history.shape[1], history.shape[2])
    block = (2 * NO, span)
    return pl.pallas_call(
        functools.partial(whole_kernel, rows_n, cols_n),
        out_shape=jax.ShapeDtypeStruct(green.shape, F32),
        in_specs=[VMEM, VMEM, pl.BlockSpec(memory_space=pl.ANY)],
        out_specs=VMEM,
        scratch_shapes=[
            pltpu.VMEM(stacked.shape, BF16),
            pltpu.SemaphoreType.DMA,
            pltpu.VMEM((NO * NO, aux), BF16),
            pltpu.VMEM((aux, NO * NO), BF16),
            pltpu.VMEM((NO * PITCH, aux), F32),
            pltpu.VMEM((2, PAIR, 2 * PAIR), BF16),
            pltpu.VMEM((2 * 2 * span * SLOTS, PAIR), F32),
            pltpu.VMEM((2 * span * SLOTS, WIDE), BF16),
            pltpu.VMEM((2, span, 2 * PAIR), BF16),
            pltpu.VMEM((span, PAIR, aux), BF16),
            pltpu.VMEM((NO * NO, times * aux), BF16),
            pltpu.VMEM((NO * NO, times * aux), BF16),
            pltpu.VMEM(green.shape, F32),
            pltpu.VMEM((steps, *block), BF16),
            pltpu.VMEM((steps, cols_n, *block), BF16),
            pltpu.VMEM((steps, rows_n, *block), BF16),
            pltpu.VMEM((steps, rows_n, *block), BF16),
            pltpu.SemaphoreType.DMA((steps, cols_n)),
            pltpu.SemaphoreType.DMA((steps, cols_n)),
            pltpu.SemaphoreType.DMA((steps, rows_n)),
            pltpu.SemaphoreType.DMA((steps, rows_n)),
        ],
        compiler_params=pltpu.CompilerParams(
            collective_id=0, has_side_effects=True, vmem_limit_bytes=62 << 20
        ),
        name="whole",
    )(green, fit, stacked)


def solution(mesh):
    in_specs = (P("groups", None, ("row", "col")), P("groups", None), P("groups", "row", "col"))
    out_specs = P("groups", None, ("row", "col"))
    return jax.shard_map(local, mesh=mesh, in_specs=in_specs, out_specs=out_specs, check_vma=False)
```
